512 devices in a mesh: kv: 4 (over x), tok: 128 (over y, z, core).
Axes of the slice: x: 4, y: 4, z: 16, core: 2. Of those that a mesh axis runs over, the one named last changes fastest.
Arguments:
- layer_input: bfloat16 [128, 512, 1536], P('tok', 'kv'), may hold values from -6 to 6
- queries: bfloat16 [128, 512, 1536], P('tok', None, 'kv'), may hold values from -80 to 80
- keys_new: bfloat16 [128, 512, 512], P('tok', None, 'kv'), may hold values from -4 to 4
- values_new: bfloat16 [128, 512, 512], P('tok', None, 'kv'), may hold values from -6 to 6
- cache_keys: bfloat16 [128, 1024, 512], P('tok', None, 'kv'), may hold values from -4 to 4
- cache_values: bfloat16 [128, 1024, 512], P('tok', None, 'kv'), may hold values from -6 to 6
- cache_length: int32 [128], P('tok'), may hold values from 128 to 1024, as said below
- cache_start: int32 [128], P('tok'), may hold values from 0 to 256, as said below
- output_proj: bfloat16 [1536, 1536], P('kv', 'tok'), may hold values from -0.15625 to 0.15625
- norm_gain: float32 [1536], replicated, may hold values from 0.1 to 1.9
- expert_routes: int32 [128, 512, 6], P('tok', 'kv'), may hold values from 0 to 63, all different within a row; in each aligned block of 128 rows (0 to 127, 128 to 255, ..., all dimensions but the last counted through in order) at most 16 rows name the same one
- route_weights: float32 [128, 512, 6], P('tok', 'kv'), may hold values from 0.05 to 0.35
- piece_gate_up: bfloat16 [128, 1536, 512], P('tok'), may hold values from -0.15625 to 0.15625
- piece_down: bfloat16 [128, 256, 1536], P('tok'), may hold values from -0.25 to 0.25
Outputs:
- layer_output: bfloat16 [128, 512, 1536], P('tok', 'kv')
The draws below stay inside these ranges and needn't reach their ends.
Inputs may be any that keep to these rules, and one draw needn't show every extreme that they name: `cache_length`: one request in every draw has exactly 1024 cached positions. cache_start of a request is at most its cache_length // 4; one request with 1024 cached positions starts at exactly 256. `expert_routes`: the 6 experts of a token are distinct; in each aligned block of 128 tokens (the tokens of one request on one index of kv) no expert is named by more than 16 tokens, a bound that some block reaches.
All inputs are finite; a program needn't handle non-finite values.
Results may differ from the reference program's by a relative error of at most 0.0046.
Values may be sent and summed in bfloat16 or wider, within the bound.
A program may use at most 64 MiB of HBM per device.

```python
import math
import jax
import jax.numpy as jnp
import numpy as np
from jax import lax

D = 1536
QH = 12
KVH = 4
HD = 128
EXPERTS = 64
EFF = 512
TOPK = 6
SPAN = 512
CACHE = 1024
CAP = 16
REQUESTS = 128
ROWS_DEV = 128
PIECE = 256
N_KV = 4


def longest_request(key):
    return jax.random.randint(jax.random.fold_in(key, 12), (), 0, REQUESTS, dtype=jnp.int32)


def cache_lengths(key):
    lengths = jax.random.randint(jax.random.fold_in(key, 11), (REQUESTS,), CACHE // 8, CACHE + 1, dtype=jnp.int32)
    return lengths.at[longest_request(key)].set(CACHE)


def cache_key_field(key):
    field = jnp.clip(jax.random.normal(jax.random.fold_in(key, 21), (REQUESTS, CACHE, KVH * HD), jnp.float32), -4.0, 4.0)
    return field


def draw_cache_length(key, part):
    return cache_lengths(key)


def draw_cache_start(key, part):
    lengths = cache_lengths(key)
    starts = jax.random.randint(jax.random.fold_in(key, 13), (REQUESTS,), 0, lengths // 4 + 1, dtype=jnp.int32)
    return starts.at[longest_request(key)].set(CACHE // 4)


def draw_cache_keys(key, part):
    return cache_key_field(key).astype(jnp.bfloat16)


def draw_queries(key, part):
    field = jnp.clip(jax.random.normal(jax.random.fold_in(key, 31), (REQUESTS, SPAN, QH * HD), jnp.float32), -4.0, 4.0)
    return field.astype(jnp.bfloat16)


def block_levels(rng, extent, shards, low, high):
    gain = 1.0
    for axis_at, shards_of in shards:
        draws = jax.random.uniform(jax.random.fold_in(jax.random.fold_in(rng, 6), axis_at), (shards_of,), jnp.float32, low / len(shards), high / len(shards))
        gain = gain * jnp.repeat(jnp.exp(draws), extent[axis_at] // shards_of).reshape((-1,) + (1,) * (len(extent) - 1 - axis_at))
    return gain


def routed_block(own_key, own, number, rows, amount, top, limit, lean):
    sequence = jax.random.permutation(own_key, amount)
    heavy_load, ordinary = shares(amount, rows * top, limit, lean, True), shares(amount, rows * top, limit, lean, False)
    places = jnp.arange(amount)

    def named(sizes, offset_by):
        used = int((sizes > 0).sum())
        fixed = max(1, used // 4)
        shifted = fixed + (places - fixed + offset_by * (used - fixed)) % max(1, amount - fixed)
        return jnp.zeros((amount,), jnp.int32).at[sequence[jnp.where(places < fixed, places, shifted)]].set(jnp.asarray(sizes, jnp.int32))

    sizes = jnp.where(number % 4 == 0, named(heavy_load, number // 4), named(ordinary, number - number // 4 - 1))
    mixed = jax.random.permutation(jax.random.fold_in(own, 3), amount)
    source_of, sink = mixed[0:amount // 2 * 2:2], mixed[1:amount // 2 * 2:2]
    slack = jnp.minimum(sizes[source_of] - 1, limit - sizes[sink]) // 2
    slack = jnp.where((source_of == sequence[0]) | (sink == sequence[0]) | (sizes[sink] == 0), 0, jnp.maximum(slack, 0))
    shifted = jax.random.randint(jax.random.fold_in(own, 4), (amount // 2,), 0, 1 << 20) % (slack + 1)
    sizes = sizes.at[source_of].add(-shifted).at[sink].add(shifted)
    items = jnp.searchsorted(jnp.cumsum(sizes), jnp.arange(rows * top), side="right").astype(jnp.int32)
    listing = items.reshape(top, rows).T
    listing = listing[jax.random.permutation(jax.random.fold_in(own, 1), rows)]
    offset_by = jax.random.randint(jax.random.fold_in(own, 2), (rows, 1), 0, top)
    return jnp.take_along_axis(listing, (jnp.arange(top)[None, :] + offset_by) % top, axis=1)


def shares(number_of, total, limit, lean, full):
    portions = [(1 << 20) // math.isqrt(grade ** lean) + 1 for grade in range(1, number_of + 1)]
    largest = limit if full else min(limit, max(-(-total // number_of), total * portions[0] // sum(portions)))
    least = 1 if total - largest >= number_of - 1 else 0
    holding, spare = [largest] + [least] * (number_of - 1), total - largest - least * (number_of - 1)
    while spare > 0:
        candidates = [i for i in range(1, number_of) if holding[i] < largest] or [i for i in range(1, number_of) if holding[i] < limit]
        mass, left = sum([portions[i] for i in candidates]), spare
        for i in candidates:
            extra = min(limit - holding[i], max(1, left * portions[i] // mass), spare)
            holding[i] = holding[i] + extra
            spare = spare - extra
    return np.array(holding)


def scatter_about(rng, shape, deviation, limit, split=(), held_as=jnp.bfloat16):
    result = jax.random.normal(rng, shape, jnp.float32) * deviation
    if len(split) > 0:
        result = block_levels(rng, shape, split, -0.22, 0.18) * result
    return jnp.clip(result, min=-limit, max=limit).astype(held_as)


def setup_inputs(seed: int = 0) -> dict:
    seeds = jax.random.split(jax.random.key(seed), 15)
    layer_input = scatter_about(seeds[0], (REQUESTS, SPAN, D), 1.0, 6.0, ((0, 128), (1, 4)))
    queries = draw_queries(jax.random.fold_in(seeds[14], 71), 0)
    keys_new = scatter_about(seeds[2], (REQUESTS, SPAN, KVH * HD), 1.0, 4.0, ((0, 128), (2, 4)))
    values_new = scatter_about(seeds[3], (REQUESTS, SPAN, KVH * HD), 1.0, 6.0, ((0, 128), (2, 4)))
    cache_keys = draw_cache_keys(jax.random.fold_in(seeds[14], 71), 0)
    cache_values = scatter_about(seeds[5], (REQUESTS, CACHE, KVH * HD), 1.0, 6.0, ((0, 128), (2, 4)))
    cache_length = draw_cache_length(jax.random.fold_in(seeds[14], 71), 0)
    cache_start = draw_cache_start(jax.random.fold_in(seeds[14], 71), 0)
    output_proj = scatter_about(seeds[8], (QH * HD, D), (QH * HD) ** -0.5, 0.15625, ((0, 4), (1, 128)))
    norm_gain = jnp.clip(1.0 + 0.18 * jax.random.normal(seeds[9], (D,), jnp.float32), 0.1, 1.9)
    expert_routes_keys = jax.random.split(jax.random.fold_in(seeds[10], 1), REQUESTS * SPAN // ROWS_DEV)
    expert_routes_turns = jax.random.permutation(jax.random.fold_in(seeds[10], 3), REQUESTS * SPAN // ROWS_DEV)
    expert_routes = jax.vmap(lambda own, number: routed_block(jax.random.fold_in(seeds[10], 2), own, number, ROWS_DEV, EXPERTS, TOPK, CAP, 2))(expert_routes_keys, expert_routes_turns).reshape((REQUESTS, SPAN, TOPK))
    route_weights = jnp.clip(0.05 + 0.29999999 * jax.random.uniform(seeds[11], (REQUESTS, SPAN, TOPK), jnp.float32) ** block_levels(seeds[11], (REQUESTS, SPAN, TOPK), ((0, 128), (1, 4)), -0.2, 0.2), 0.05, 0.35)
    piece_gate_up = scatter_about(seeds[12], (2 * EXPERTS, D, 2 * PIECE), D ** -0.5, 0.15625, ((0, 128),))
    piece_down = scatter_about(seeds[13], (2 * EXPERTS, PIECE, D), EFF ** -0.5, 0.25, ((0, 128),))
    return {"layer_input": layer_input, "queries": queries, "keys_new": keys_new, "values_new": values_new, "cache_keys": cache_keys, "cache_values": cache_values, "cache_length": cache_length, "cache_start": cache_start, "output_proj": output_proj, "norm_gain": norm_gain, "expert_routes": expert_routes, "route_weights": route_weights, "piece_gate_up": piece_gate_up, "piece_down": piece_down}


def visible_mask(length, first_visible, span_rows, cached):
    cache_pos = jnp.arange(cached, dtype=jnp.int32)
    cache_ok = jnp.logical_and(cache_pos >= first_visible, cache_pos < length)
    position = jnp.arange(span_rows, dtype=jnp.int32)
    causal = position[None, :] <= position[:, None]
    return jnp.concatenate([jnp.broadcast_to(cache_ok[None, :], (span_rows, cached)), causal], axis=1)

def attend_heads(query_rows, all_keys, all_values, allowed, per_group):
    head_count = query_rows.shape[1] // HD
    score_scale = HD ** (-0.5)
    results = []
    for head_index in range(head_count):
        group_index = head_index // per_group
        query_block = query_rows[:, head_index * HD:(head_index + 1) * HD]
        key_block = all_keys[:, group_index * HD:(group_index + 1) * HD]
        value_block = all_values[:, group_index * HD:(group_index + 1) * HD]
        scores = jnp.dot(query_block, key_block.T, preferred_element_type=jnp.float32) * score_scale
        scores = jnp.where(allowed, scores, -1e+30)
        largest = lax.optimization_barrier(jnp.max(scores, axis=1, keepdims=True))
        exponent = jnp.exp(scores - largest)
        attention_weights = (exponent / lax.optimization_barrier(jnp.sum(exponent, axis=1, keepdims=True))).astype(jnp.bfloat16)
        results.append(jnp.dot(attention_weights, value_block, preferred_element_type=jnp.float32).astype(jnp.bfloat16))
    return jnp.concatenate(results, axis=1)

def slot_places(route_rows):
    onehot = (route_rows[..., None] == jnp.arange(EXPERTS, dtype=jnp.int32)).astype(jnp.int32)
    rank_table = jnp.cumsum(onehot, axis=-2) - 1
    slot_index = lax.optimization_barrier(jnp.sum(onehot * rank_table, axis=-1))
    return route_rows * CAP + slot_index

def reference(layer_input, queries, keys_new, values_new, cache_keys, cache_values, cache_length, cache_start, output_proj, norm_gain, expert_routes, route_weights, piece_gate_up, piece_down):
    per_group = QH // KVH

    def one_request(packed):
        query_rows, new_keys, new_values, old_keys, old_values, length, first_visible = packed
        allowed = visible_mask(length, first_visible, SPAN, CACHE)
        all_keys = jnp.concatenate([old_keys, new_keys], axis=0)
        all_values = jnp.concatenate([old_values, new_values], axis=0)
        return attend_heads(query_rows, all_keys, all_values, allowed, per_group)
    attended = lax.map(one_request, (queries, keys_new, values_new, cache_keys, cache_values, cache_length, cache_start))
    token_count = REQUESTS * SPAN
    attention = jnp.dot(attended.reshape(token_count, QH * HD), output_proj, preferred_element_type=jnp.float32)
    residual = layer_input.reshape(token_count, D).astype(jnp.float32) + attention
    normed = (residual * lax.rsqrt(lax.optimization_barrier(jnp.mean(residual * residual, axis=1, keepdims=True)) + 1e-05) * norm_gain).astype(jnp.bfloat16)
    block_rows = SPAN // N_KV
    block_count = REQUESTS * N_KV
    pairs = block_rows * TOPK
    flat_routes = expert_routes.reshape(block_count, pairs)
    flat_weights = route_weights.reshape(block_count, pairs)
    places = slot_places(flat_routes)
    block_ids = jnp.arange(block_count, dtype=jnp.int32)[:, None]
    row_of_pair = jnp.broadcast_to((jnp.arange(pairs, dtype=jnp.int32) // TOPK)[None, :], (block_count, pairs))
    source_table = jnp.full((block_count, EXPERTS * CAP), block_rows, jnp.int32).at[block_ids, places].set(row_of_pair)
    weight_table = jnp.zeros((block_count, EXPERTS * CAP), jnp.float32).at[block_ids, places].set(flat_weights)
    padded = jnp.concatenate([normed.reshape(block_count, block_rows, D), jnp.zeros((block_count, 1, D), jnp.bfloat16)], axis=1)

    def expert_step(accumulated, expert):
        start_col = expert * CAP
        pick_rows = lax.dynamic_slice_in_dim(source_table, start_col, CAP, 1)
        scales = lax.dynamic_slice_in_dim(weight_table, start_col, CAP, 1)
        wide_picks = jnp.broadcast_to(pick_rows[:, :, None], (block_count, CAP, D))
        chosen = jnp.take_along_axis(padded, wide_picks, axis=1).reshape(block_count * CAP, D)
        merged = jnp.zeros((block_count * CAP, D), jnp.float32)
        for half_index in range(2):
            piece_index = half_index * EXPERTS + expert
            weights_in = lax.dynamic_index_in_dim(piece_gate_up, piece_index, 0, keepdims=False)
            weights_out = lax.dynamic_index_in_dim(piece_down, piece_index, 0, keepdims=False)
            gate_up = jnp.dot(chosen, weights_in, preferred_element_type=jnp.float32)
            hidden = (jax.nn.silu(gate_up[:, :PIECE]) * gate_up[:, PIECE:]).astype(jnp.bfloat16)
            produced = lax.optimization_barrier(jnp.dot(hidden, weights_out, preferred_element_type=jnp.float32).astype(jnp.bfloat16))
            merged = merged + produced.astype(jnp.float32)
        contrib = merged.reshape(block_count, CAP, D) * scales[:, :, None]
        return (accumulated.at[block_ids, pick_rows].add(contrib), None)
    initial = jnp.zeros((block_count, block_rows + 1, D), jnp.float32)
    accumulated, unused = lax.scan(expert_step, initial, jnp.arange(EXPERTS, dtype=jnp.int32))
    routed_sum = accumulated[:, :block_rows, :].reshape(token_count, D)
    return (residual + routed_sum).astype(jnp.bfloat16).reshape(REQUESTS, SPAN, D)
```

```python
import jax
import jax.numpy as jnp
from jax import lax
from jax.sharding import PartitionSpec as P

HD = 128
EXPERTS = 64
TOPK = 6
CAP = 16


def visible_mask(length, first_visible, span_rows, cached):
    cache_pos = jnp.arange(cached, dtype=jnp.int32)
    cache_ok = jnp.logical_and(cache_pos >= first_visible, cache_pos < length)
    position = jnp.arange(span_rows, dtype=jnp.int32)
    causal = position[None, :] <= position[:, None]
    return jnp.concatenate(
        [jnp.broadcast_to(cache_ok[None, :], (span_rows, cached)), causal], axis=1
    )


def attend_heads(query_rows, all_keys, all_values, allowed):
    head_count = query_rows.shape[1] // HD
    score_scale = HD ** (-0.5)
    results = []
    for head_index in range(head_count):
        query_block = query_rows[:, head_index * HD : (head_index + 1) * HD]
        scores = jnp.dot(query_block, all_keys.T, preferred_element_type=jnp.float32) * score_scale
        scores = jnp.where(allowed, scores, -1e30)
        largest = jnp.max(scores, axis=1, keepdims=True)
        exponent = jnp.exp(scores - largest)
        attention_weights = (exponent / jnp.sum(exponent, axis=1, keepdims=True)).astype(
            jnp.bfloat16
        )
        results.append(
            jnp.dot(attention_weights, all_values, preferred_element_type=jnp.float32).astype(
                jnp.bfloat16
            )
        )
    return jnp.concatenate(results, axis=1)


def tok_groups(members):
    chips_z = members // 8
    along_z = [
        [(y * chips_z + z) * 2 + core for z in range(chips_z)]
        for y in range(4)
        for core in range(2)
    ]
    across = [
        [(y * chips_z + z) * 2 + core for y in range(4) for core in range(2)]
        for z in range(chips_z)
    ]
    return along_z, across


def slot_tables(table, first_expert):
    blocks, _, rows = table.shape
    experts = jnp.stack(
        [first_expert, first_expert + 1, first_expert + 32, first_expert + 33]
    ).astype(jnp.float32)
    named = table[:, None, :TOPK, :] == experts[None, :, None, None]
    member = jnp.any(named, axis=2)
    weight = jnp.sum(jnp.where(named, table[:, None, TOPK:, :], 0.0), axis=2)
    earlier = (
        jnp.arange(rows, dtype=jnp.int32)[:, None] < jnp.arange(rows, dtype=jnp.int32)[None, :]
    ).astype(jnp.bfloat16)
    rank = jnp.dot(
        member.astype(jnp.bfloat16).reshape(blocks * 4, rows),
        earlier,
        preferred_element_type=jnp.float32,
    ).reshape(blocks, 4, rows)
    slots = jnp.arange(CAP, dtype=jnp.int32).astype(jnp.float32)
    chosen = jnp.logical_and(
        member[:, :, None, :], rank[:, :, None, :] == slots[None, None, :, None]
    )
    slot_weight = jnp.sum(jnp.where(chosen, weight[:, :, None, :], 0.0), axis=3)
    return chosen.astype(jnp.bfloat16), slot_weight


def run_experts(normed_rows, chosen, slot_weight, gate_up, down):
    blocks, rows, width = normed_rows.shape
    grouped = jnp.einsum(
        "bect,btd->ebcd", chosen, normed_rows, preferred_element_type=jnp.float32
    ).astype(jnp.bfloat16)
    grouped = grouped.reshape(4, blocks * CAP, width)
    half = down.shape[1]
    produced = []
    for expert in range(4):
        total = None
        for part in range(2):
            piece = part * 4 + expert
            both = jnp.dot(grouped[expert], gate_up[piece], preferred_element_type=jnp.float32)
            hidden = (jax.nn.silu(both[:, :half]) * both[:, half:]).astype(jnp.bfloat16)
            out = jnp.dot(hidden, down[piece], preferred_element_type=jnp.float32)
            total = out if total is None else total + out
        scale = slot_weight[:, expert, :].reshape(blocks * CAP, 1)
        produced.append((total * scale).astype(jnp.bfloat16).reshape(blocks, CAP, width))
    stacked = jnp.stack(produced, axis=1)
    return jnp.einsum(
        "bect,becd->btd", chosen, stacked, preferred_element_type=jnp.float32
    ).astype(jnp.bfloat16)


def on_device(
    layer_input,
    queries,
    keys_new,
    values_new,
    cache_keys,
    cache_values,
    cache_length,
    cache_start,
    output_proj,
    norm_gain,
    expert_routes,
    route_weights,
    piece_gate_up,
    piece_down,
):
    span_rows = queries.shape[1]
    cached = cache_keys.shape[1]
    allowed = visible_mask(cache_length[0], cache_start[0], span_rows, cached)
    all_keys = jnp.concatenate([cache_keys[0], keys_new[0]], axis=0)
    all_values = jnp.concatenate([cache_values[0], values_new[0]], axis=0)
    attended = attend_heads(queries[0], all_keys, all_values, allowed)
    members = lax.axis_size("tok")
    along_z, across = tok_groups(members)
    chips_z = members // 8
    rows_out, cols_own = output_proj.shape
    model_width = layer_input.shape[2]
    table = jnp.concatenate(
        [expert_routes[0].astype(jnp.float32).T, route_weights[0].T], axis=0
    )
    table = lax.all_gather(table, "tok", axis=0, axis_index_groups=along_z)
    proj = lax.all_gather(output_proj.T, "tok", axis=0, axis_index_groups=along_z)
    proj = lax.all_gather(proj, "tok", axis=0, axis_index_groups=across)
    proj = (
        proj.reshape(4, 2, chips_z, cols_own, rows_out)
        .transpose(0, 2, 1, 3, 4)
        .reshape(model_width, rows_out)
    )
    gate_up = lax.all_gather(piece_gate_up[0], "tok", axis=0, axis_index_groups=across)
    down = lax.all_gather(piece_down[0], "tok", axis=0, axis_index_groups=across)
    partial_sums = lax.dot_general(
        attended, proj, (((1,), (1,)), ((), ())), preferred_element_type=jnp.float32
    )
    attention = lax.psum_scatter(partial_sums, "kv", scatter_dimension=0, tiled=True)
    residual = layer_input[0].astype(jnp.float32) + attention
    normed = (
        residual
        * lax.rsqrt(jnp.mean(residual * residual, axis=1, keepdims=True) + 1e-05)
        * norm_gain
    ).astype(jnp.bfloat16)
    first_expert = 2 * (lax.axis_index("tok") // 2 % chips_z)
    chosen, slot_weight = slot_tables(table, first_expert)
    normed_rows = lax.all_gather(normed, "tok", axis=0, axis_index_groups=along_z)
    sums = run_experts(normed_rows, chosen, slot_weight, gate_up, down)
    routed_sum = lax.psum_scatter(
        sums, "tok", scatter_dimension=0, axis_index_groups=along_z, tiled=False
    )
    return (residual + routed_sum.astype(jnp.float32)).astype(jnp.bfloat16)[None]


def solution(mesh):
    return jax.shard_map(
        on_device,
        mesh=mesh,
        in_specs=(
            P("tok", "kv", None),
            P("tok", None, "kv"),
            P("tok", None, "kv"),
            P("tok", None, "kv"),
            P("tok", None, "kv"),
            P("tok", None, "kv"),
            P("tok"),
            P("tok"),
            P("kv", "tok"),
            P(),
            P("tok", "kv", None),
            P("tok", "kv", None),
            P("tok", None, None),
            P("tok", None, None),
        ),
        out_specs=P("tok", "kv", None),
        check_vma=False,
    )
```

```python
import functools

import jax
import jax.numpy as jnp
from jax import lax
from jax.experimental import pallas as pl
from jax.experimental.pallas import tpu as pltpu
from jax.sharding import PartitionSpec as P

HD = 128
EXPERTS = 64
TOPK = 6
CAP = 16


def visible_mask(length, first_visible, span_rows, cached):
    cache_pos = jnp.arange(cached, dtype=jnp.int32)
    cache_ok = jnp.logical_and(cache_pos >= first_visible, cache_pos < length)
    position = jnp.arange(span_rows, dtype=jnp.int32)
    causal = position[None, :] <= position[:, None]
    return jnp.concatenate(
        [jnp.broadcast_to(cache_ok[None, :], (span_rows, cached)), causal], axis=1
    )


def attend_heads(query_rows, all_keys, all_values, allowed):
    head_count = query_rows.shape[1] // HD
    score_scale = HD ** (-0.5)
    results = []
    for head_index in range(head_count):
        query_block = query_rows[:, head_index * HD : (head_index + 1) * HD]
        scores = jnp.dot(query_block, all_keys.T, preferred_element_type=jnp.float32) * score_scale
        scores = jnp.where(allowed, scores, -1e30)
        largest = jnp.max(scores, axis=1, keepdims=True)
        exponent = jnp.exp(scores - largest)
        attention_weights = (exponent / jnp.sum(exponent, axis=1, keepdims=True)).astype(
            jnp.bfloat16
        )
        results.append(
            jnp.dot(attention_weights, all_values, preferred_element_type=jnp.float32).astype(
                jnp.bfloat16
            )
        )
    return jnp.concatenate(results, axis=1)


def tok_groups(members):
    chips_z = members // 8
    return [
        [(y * chips_z + z) * 2 + core for y in range(4) for core in range(2)]
        for z in range(chips_z)
    ]


def slot_tables(table, first_expert):
    blocks, _, rows = table.shape
    experts = jnp.stack(
        [first_expert, first_expert + 1, first_expert + 32, first_expert + 33]
    ).astype(jnp.float32)
    named = table[:, None, :TOPK, :] == experts[None, :, None, None]
    member = jnp.any(named, axis=2)
    weight = jnp.sum(jnp.where(named, table[:, None, TOPK:, :], 0.0), axis=2)
    earlier = (
        jnp.arange(rows, dtype=jnp.int32)[:, None] < jnp.arange(rows, dtype=jnp.int32)[None, :]
    ).astype(jnp.bfloat16)
    rank = jnp.dot(
        member.astype(jnp.bfloat16).reshape(blocks * 4, rows),
        earlier,
        preferred_element_type=jnp.float32,
    ).reshape(blocks, 4, rows)
    slots = jnp.arange(CAP, dtype=jnp.int32).astype(jnp.float32)
    chosen = jnp.logical_and(
        member[:, :, None, :], rank[:, :, None, :] == slots[None, None, :, None]
    )
    slot_weight = jnp.sum(jnp.where(chosen, weight[:, :, None, :], 0.0), axis=3)
    return chosen.astype(jnp.bfloat16), slot_weight


def run_experts(normed_rows, chosen, slot_weight, gate_up, down):
    blocks, rows, width = normed_rows.shape
    grouped = jnp.einsum(
        "bect,btd->ebcd", chosen, normed_rows, preferred_element_type=jnp.float32
    ).astype(jnp.bfloat16)
    grouped = grouped.reshape(4, blocks * CAP, width)
    half = down.shape[1]
    produced = []
    for expert in range(4):
        total = None
        for part in range(2):
            piece = part * 4 + expert
            both = jnp.dot(grouped[expert], gate_up[piece], preferred_element_type=jnp.float32)
            hidden = (jax.nn.silu(both[:, :half]) * both[:, half:]).astype(jnp.bfloat16)
            out = jnp.dot(hidden, down[piece], preferred_element_type=jnp.float32)
            total = out if total is None else total + out
        scale = slot_weight[:, expert, :].reshape(blocks * CAP, 1)
        produced.append((total * scale).astype(jnp.bfloat16).reshape(blocks, CAP, width))
    stacked = jnp.stack(produced, axis=1)
    return jnp.einsum(
        "bect,becd->btd", chosen, stacked, preferred_element_type=jnp.float32
    ).astype(jnp.bfloat16)


MESH = pl.DeviceIdType.MESH


def spot(chips_z):
    here = lax.axis_index("tok")
    y, z, core = here // (2 * chips_z), (here // 2) % chips_z, here % 2

    def index(y, z, core):
        return (y * chips_z + z) * 2 + core

    return y, z, core, index


def greet(peers):
    barrier = pltpu.get_barrier_semaphore()
    for peer in peers:
        pl.semaphore_signal(barrier, inc=1, device_id=peer, device_id_type=MESH)
    pl.semaphore_wait(barrier, len(peers))


def params_kernel(chips_z, shard_ref, table_ref, proj_ref, tables_ref,
                  zs, zr, ts, tr, ys, yr, cs, cr):
    y, z, core, index = spot(chips_z)
    far = [(z + d) % chips_z for d in range(1, chips_z)]
    beside = [(y + d) % 4 for d in range(1, 4)]
    partner = {"tok": index(y, z, 1 - core)}
    peers = [{"tok": index(y, other, core)} for other in far]
    peers += [{"tok": index(other, z, core)} for other in beside] + [partner]
    greet(peers)

    def push(src, dst, send, recv, target):
        return pltpu.make_async_remote_copy(
            src_ref=src, dst_ref=dst, send_sem=send, recv_sem=recv,
            device_id=target, device_id_type=MESH,
        )

    shards = []
    order = sorted(range(chips_z - 1), key=lambda d: -min(d + 1, chips_z - 1 - d))
    for d in order:
        shards.append(
            push(shard_ref, proj_ref.at[core, y, z], zs.at[d], zr.at[d], peers[d])
        )
        shards[-1].start()
    for d in order:
        shards.append(push(table_ref, tables_ref.at[z], ts.at[d], tr.at[d], peers[d]))
        shards[-1].start()
    proj_ref[core, y, z] = shard_ref[...]
    tables_ref[z] = table_ref[...]
    for copy in shards[: chips_z - 1]:
        copy.wait_recv()
    columns = []
    for d, other in enumerate(beside):
        block = proj_ref.at[core, y]
        columns.append(
            push(block, block, ys.at[d], yr.at[d], {"tok": index(other, z, core)})
        )
        columns[-1].start()
    halves = []
    for d in range(4):
        if d > 0:
            columns[d - 1].wait_recv()
        block = proj_ref.at[core, (y + 4 - d) % 4]
        halves.append(push(block, block, cs.at[d], cr.at[d], partner))
        halves[-1].start()
    for copy in shards[chips_z - 1 :]:
        copy.wait_recv()
    for copy in halves:
        copy.wait_recv()
    for copy in shards + columns + halves:
        copy.wait_send()


def gather_params(shard, table, chips_z):
    cols, rows = shard.shape
    dma = pltpu.SemaphoreType.DMA
    vmem = pl.BlockSpec(memory_space=pltpu.VMEM)
    return pl.pallas_call(
        functools.partial(params_kernel, chips_z),
        out_shape=(
            jax.ShapeDtypeStruct((2, 4, chips_z, cols, rows), shard.dtype),
            jax.ShapeDtypeStruct((chips_z,) + table.shape, table.dtype),
        ),
        in_specs=[vmem, vmem],
        out_specs=(vmem, vmem),
        scratch_shapes=[dma((chips_z - 1,))] * 4 + [dma((3,))] * 2 + [dma((4,))] * 2,
        compiler_params=pltpu.CompilerParams(collective_id=0, has_side_effects=True),
    )(shard, table)


def ring_chunks(chips_z, step):
    if step < chips_z // 2 - 1:
        return [(0, 0), (1, 1), (0, 1), (1, 0)]
    return [(0, 0), (1, 1)]


def norm_kernel(chips_z, kv_count, parts_ref, input_ref, gain_ref, residual_ref, rows_ref,
                got, xs, xr, zs, zr):
    y, z, core, index = spot(chips_z)
    me = lax.axis_index("kv")
    half = input_ref.shape[0] // 2
    owners = [(me + d) % kv_count for d in range(1, kv_count)]
    steps = ((z + 1) % chips_z, (z + chips_z - 1) % chips_z)
    sides = [{"tok": index(y, other, core)} for other in steps]
    greet([{"kv": other} for other in owners] + sides)
    shares = {}
    for chunk in range(2):
        span = pl.ds(chunk * half, half)
        for d in sorted(range(kv_count - 1), key=lambda d: -min(d + 1, kv_count - 1 - d)):
            shares[d, chunk] = pltpu.make_async_remote_copy(
                src_ref=parts_ref.at[owners[d], span], dst_ref=got.at[d, span],
                send_sem=xs.at[d, chunk], recv_sem=xr.at[d, chunk],
                device_id={"kv": owners[d]}, device_id_type=MESH,
            )
            shares[d, chunk].start()

    moves = {}

    def move(direction, step, chunk):
        block = (z + chips_z - step) % chips_z if direction == 0 else (z + step) % chips_z
        ref = rows_ref.at[block, pl.ds(chunk * half, half)]
        moves[direction, step, chunk] = pltpu.make_async_remote_copy(
            src_ref=ref, dst_ref=ref,
            send_sem=zs.at[direction, step, chunk], recv_sem=zr.at[direction, step, chunk],
            device_id=sides[direction], device_id_type=MESH,
        )
        moves[direction, step, chunk].start()

    for chunk in range(2):
        for d in range(kv_count - 1):
            shares[d, chunk].wait_recv()

        def tile(i, carry):
            span = pl.ds(pl.multiple_of(chunk * half + i * 16, 16), 16)
            total = parts_ref[me, span].astype(jnp.float32)
            for d in range(kv_count - 1):
                total = total + got[d, span].astype(jnp.float32)
            total = total + input_ref[span].astype(jnp.float32)
            residual_ref[span] = total
            mean = jnp.mean(total * total, axis=1, keepdims=True)
            rows_ref[z, span] = (total * lax.rsqrt(mean + 1e-05) * gain_ref[...]).astype(
                jnp.bfloat16
            )
            return carry

        lax.fori_loop(0, half // 16, tile, 0)
        for direction, part in ring_chunks(chips_z, 0):
            if part == chunk:
                move(direction, 0, chunk)
    for step in range(1, chips_z // 2):
        for direction, chunk in ring_chunks(chips_z, step):
            moves[direction, step - 1, chunk].wait_recv()
            move(direction, step, chunk)
    last = chips_z // 2 - 1
    for direction, chunk in ((0, 1), (1, 0)):
        moves[direction, last - 1, chunk].wait_recv()
    for direction, chunk in ring_chunks(chips_z, last):
        moves[direction, last, chunk].wait_recv()
    for copy in list(shares.values()) + list(moves.values()):
        copy.wait_send()


def norm_and_gather(parts, layer_rows, gain, chips_z):
    kv_count, rows, width = parts.shape
    dma = pltpu.SemaphoreType.DMA
    vmem = pl.BlockSpec(memory_space=pltpu.VMEM)
    return pl.pallas_call(
        functools.partial(norm_kernel, chips_z, kv_count),
        out_shape=(
            jax.ShapeDtypeStruct((rows, width), jnp.float32),
            jax.ShapeDtypeStruct((chips_z, rows, width), jnp.bfloat16),
        ),
        in_specs=[vmem] * 3,
        out_specs=(vmem, vmem),
        scratch_shapes=[pltpu.VMEM((kv_count - 1, rows, width), jnp.bfloat16)]
        + [dma((kv_count - 1, 2))] * 2
        + [dma((2, chips_z // 2, 2))] * 2,
        compiler_params=pltpu.CompilerParams(collective_id=1, has_side_effects=True),
    )(parts, layer_rows, gain)


def return_kernel(chips_z, sums_ref, residual_ref, out_ref, arrived, ss, sr):
    y, z, core, index = spot(chips_z)
    half = residual_ref.shape[0] // 2
    reach = chips_z // 2
    steps = ((z + 1) % chips_z, (z + chips_z - 1) % chips_z)
    sides = [{"tok": index(y, other, core)} for other in steps]
    greet(sides)
    moves = {}
    for step in range(reach):
        for direction, chunk in ring_chunks(chips_z, reach - 1 - step):
            ahead = reach - step
            target = (z + ahead) % chips_z if direction == 0 else (z + chips_z - ahead) % chips_z
            span = pl.ds(chunk * half, half)
            source = sums_ref.at[target, span]
            if (direction, step - 1, chunk) in moves:
                moves[direction, step - 1, chunk].wait_recv()
                held = arrived.at[direction, step - 1]
                held[span] = (
                    held[span].astype(jnp.float32)
                    + sums_ref[target, span].astype(jnp.float32)
                ).astype(jnp.bfloat16)
                source = arrived.at[direction, step - 1, span]
            moves[direction, step, chunk] = pltpu.make_async_remote_copy(
                src_ref=source, dst_ref=arrived.at[direction, step, span],
                send_sem=ss.at[direction, step, chunk], recv_sem=sr.at[direction, step, chunk],
                device_id=sides[direction], device_id_type=MESH,
            )
            moves[direction, step, chunk].start()
    for chunk in range(2):
        span = pl.ds(chunk * half, half)
        total = residual_ref[span] + sums_ref[z, span].astype(jnp.float32)
        for direction in range(2):
            moves[direction, reach - 1, chunk].wait_recv()
            total = total + arrived[direction, reach - 1, span].astype(jnp.float32)
        out_ref[span] = total.astype(jnp.bfloat16)
    for copy in moves.values():
        copy.wait_send()


def return_sums(sums, residual, chips_z):
    rows, width = residual.shape
    dma = pltpu.SemaphoreType.DMA
    vmem = pl.BlockSpec(memory_space=pltpu.VMEM)
    return pl.pallas_call(
        functools.partial(return_kernel, chips_z),
        out_shape=jax.ShapeDtypeStruct((rows, width), jnp.bfloat16),
        in_specs=[vmem, vmem],
        out_specs=vmem,
        scratch_shapes=[pltpu.VMEM((2, chips_z // 2, rows, width), jnp.bfloat16)]
        + [dma((2, chips_z // 2, 2))] * 2,
        compiler_params=pltpu.CompilerParams(collective_id=2, has_side_effects=True),
    )(sums, residual)


def on_device(
    layer_input,
    queries,
    keys_new,
    values_new,
    cache_keys,
    cache_values,
    cache_length,
    cache_start,
    output_proj,
    norm_gain,
    expert_routes,
    route_weights,
    piece_gate_up,
    piece_down,
):
    span_rows = queries.shape[1]
    cached = cache_keys.shape[1]
    allowed = visible_mask(cache_length[0], cache_start[0], span_rows, cached)
    all_keys = jnp.concatenate([cache_keys[0], keys_new[0]], axis=0)
    all_values = jnp.concatenate([cache_values[0], values_new[0]], axis=0)
    attended = attend_heads(queries[0], all_keys, all_values, allowed)
    members = lax.axis_size("tok")
    kv_count = lax.axis_size("kv")
    across = tok_groups(members)
    chips_z = members // 8
    rows_out, cols_own = output_proj.shape
    model_width = layer_input.shape[2]
    gate_up = lax.all_gather(piece_gate_up[0], "tok", axis=0, axis_index_groups=across)
    down = lax.all_gather(piece_down[0], "tok", axis=0, axis_index_groups=across)
    table = jnp.concatenate(
        [expert_routes[0].astype(jnp.float32).T, route_weights[0].T], axis=0
    )
    proj, table = gather_params(output_proj.T, table, chips_z)
    proj = (
        proj.reshape(2, 4, chips_z, cols_own, rows_out)
        .transpose(1, 2, 0, 3, 4)
        .reshape(model_width, rows_out)
    )
    partial_sums = lax.dot_general(
        attended, proj, (((1,), (1,)), ((), ())), preferred_element_type=jnp.float32
    ).astype(jnp.bfloat16)
    residual, normed_rows = norm_and_gather(
        partial_sums.reshape(kv_count, span_rows // kv_count, model_width),
        layer_input[0],
        norm_gain[None],
        chips_z,
    )
    first_expert = 2 * (lax.axis_index("tok") // 2 % chips_z)
    chosen, slot_weight = slot_tables(table, first_expert)
    sums = run_experts(normed_rows, chosen, slot_weight, gate_up, down)
    return return_sums(sums, residual, chips_z)[None]


def solution(mesh):
    return jax.shard_map(
        on_device,
        mesh=mesh,
        in_specs=(
            P("tok", "kv", None),
            P("tok", None, "kv"),
            P("tok", None, "kv"),
            P("tok", None, "kv"),
            P("tok", None, "kv"),
            P("tok", None, "kv"),
            P("tok"),
            P("tok"),
            P("kv", "tok"),
            P(),
            P("tok", "kv", None),
            P("tok", "kv", None),
            P("tok", None, None),
            P("tok", None, None),
        ),
        out_specs=P("tok", "kv", None),
        check_vma=False,
    )
```
